512 devices in a mesh: ctx: 32 (over z, y_lo), head: 16 (over y_hi, x, core).
Axes of the slice: x: 4, y: 4 (y_hi: 2, y_lo: 2; y = y_hi * 2 + y_lo), z: 16, core: 2. Of those that a mesh axis runs over, the one named last changes fastest.
Arguments:
- query: bfloat16 [65536, 1024], P(('ctx', 'head')), may hold values from -7 to 7
- key: bfloat16 [65536, 1024], P(('ctx', 'head')), may hold values from -7 to 7
- value: bfloat16 [65536, 1024], P(('ctx', 'head')), may hold values from -6 to 6
- grad_out: bfloat16 [65536, 1024], P(('ctx', 'head')), may hold values from -6 to 6
- neighbour: int32 [512, 8], replicated, may hold values from 0 to 511, as said below
- counts: int32 [512], replicated, may hold values from 1 to 8, as said below
Outputs:
- attn_out: bfloat16 [65536, 1024], P(('ctx', 'head'))
- grad_query: bfloat16 [65536, 1024], P(('ctx', 'head'))
- grad_key: bfloat16 [65536, 1024], P(('ctx', 'head'))
- grad_value: bfloat16 [65536, 1024], P(('ctx', 'head'))
The draws below stay inside these ranges and needn't reach their ends.
Inputs may be any that keep to these rules, and one draw needn't show every extreme that they name: `neighbour`: row b lists key blocks for query block b: its first entry is b itself, and every entry lies within 32 blocks of b in the periodic block order; some row has an entry exactly 32 blocks ahead, and some row one exactly that far behind. Query block b uses the first counts[b] slots of its row; some block uses all 8 slots and some only one.
All inputs are finite; a program needn't handle non-finite values.
Results may differ from the reference program's by a relative error of at most 0.0083.
Values may be sent and summed in bfloat16 or wider, within the bound.
No kernel may reach another device: no remote copies, remote signals or barrier semaphores. Data moves between devices by JAX's collectives and lax.ppermute only.
A program may use at most 64 MiB of HBM per device.

```python
import math
import jax
import jax.numpy as jnp
from jax import lax

H = 16
E = 64
D = 1024
BLK = 128
NNB = 8
REACH = 2
SEQ = 65536
BPS = 16
NB = 512
N_CTX = 32


def paired_fields(key):
    base = jax.random.fold_in(key, 11)
    first_key, second_key = jax.random.split(base, 2)
    first = jax.random.truncated_normal(first_key, -4.0, 4.0, (SEQ, D), jnp.float32)
    second = jax.random.truncated_normal(second_key, -4.0, 4.0, (SEQ, D), jnp.float32)
    return (first, second)


def draw_query(key, part):
    return paired_fields(key)[0].astype(jnp.bfloat16)


def draw_key(key, part):
    return paired_fields(key)[1].astype(jnp.bfloat16)


def draw_neighbour(key, part):
    offset_key, pick_key = jax.random.split(jax.random.fold_in(key, 23), 2)
    span = REACH * BPS
    offsets = jax.random.randint(offset_key, (NB, NNB), -span, span + 1, jnp.int32)
    offsets = offsets.at[:, 0].set(0)
    chosen = jax.random.randint(pick_key, (), 0, NB, jnp.int32)
    offsets = offsets.at[chosen, 1].set(span)
    offsets = offsets.at[(chosen + 1) % NB, 1].set(-span)
    rows = jnp.arange(NB, dtype=jnp.int32)[:, None]
    return jnp.mod(rows + offsets, NB).astype(jnp.int32)


def draw_counts(key, part):
    count_key, pick_key = jax.random.split(jax.random.fold_in(key, 37), 2)
    drawn = jax.random.randint(count_key, (NB,), 1, NNB + 1, jnp.int32)
    chosen = jax.random.randint(pick_key, (), 0, NB, jnp.int32)
    drawn = drawn.at[chosen].set(NNB)
    drawn = drawn.at[(chosen + 1) % NB].set(1)
    return drawn.astype(jnp.int32)


def steps_of(stream_key, extent, pieces, smallest, top_value):
    factor_of = 1.0
    for dim, shards_of in pieces:
        steps = jax.random.uniform(jax.random.fold_in(jax.random.fold_in(stream_key, 6), dim), (shards_of,), jnp.float32, smallest / len(pieces), top_value / len(pieces))
        factor_of = factor_of * jnp.repeat(jnp.exp(steps), extent[dim] // shards_of).reshape((-1,) + (1,) * (len(extent) - 1 - dim))
    return factor_of


def gaussian(rng, shape, spread, most, cuts=(), kind=jnp.bfloat16):
    values = jax.random.normal(rng, shape, jnp.float32) * spread
    if len(cuts) > 0:
        values = steps_of(rng, shape, cuts, -0.22, 0.18) * values
    return jnp.clip(values, min=-most, max=most).astype(kind)


def setup_inputs(seed: int = 0) -> dict:
    streams_of = jax.random.split(jax.random.key(seed), 7)
    return {
        "query": draw_query(jax.random.fold_in(streams_of[6], 71), 0),
        "key": draw_key(jax.random.fold_in(streams_of[6], 71), 0),
        "value": gaussian(streams_of[2], (SEQ, D), 1.0, 6.0, ((0, 512),)),
        "grad_out": gaussian(streams_of[3], (SEQ, D), 1.0, 6.0, ((0, 512),)),
        "neighbour": draw_neighbour(jax.random.fold_in(streams_of[6], 71), 0),
        "counts": draw_counts(jax.random.fold_in(streams_of[6], 71), 0),
    }


def attend_blocks(queries, cotangent, keys_sel, values_sel, usable):
    scale_factor = 1.0 / math.sqrt(queries.shape[-1])
    query_f = queries.astype(jnp.float32)
    grad_f = cotangent.astype(jnp.float32)
    key_f = keys_sel.astype(jnp.float32)
    value_f = values_sel.astype(jnp.float32)
    scores = jnp.einsum('rie,rjte->rijt', query_f, key_f) * scale_factor
    allowed = usable[:, None, :, None]
    masked = jnp.where(allowed, scores, -1e+30)
    highest = lax.optimization_barrier(jnp.max(masked, axis=(2, 3), keepdims=True))
    raised = jnp.where(allowed, jnp.exp(masked - highest), 0.0)
    total = lax.optimization_barrier(jnp.sum(raised, axis=(2, 3), keepdims=True))
    probability = raised / total
    weights = probability.astype(jnp.bfloat16)
    weights_f = weights.astype(jnp.float32)
    out_rows = jnp.einsum('rijt,rjte->rie', weights_f, value_f).astype(jnp.bfloat16)
    dprob = jnp.einsum('rie,rjte->rijt', grad_f, value_f)
    row_delta = lax.optimization_barrier(jnp.sum(probability * dprob, axis=(2, 3), keepdims=True))
    dscore = (probability * (dprob - row_delta) * scale_factor).astype(jnp.bfloat16)
    dscore_f = dscore.astype(jnp.float32)
    dquery = jnp.einsum('rijt,rjte->rie', dscore_f, key_f).astype(jnp.bfloat16)
    dkey_part = jnp.einsum('rijt,rie->rjte', dscore_f, query_f)
    dvalue_part = jnp.einsum('rijt,rie->rjte', weights_f, grad_f)
    return (out_rows, dquery, dkey_part, dvalue_part)

def split_heads(array, seq_len):
    return array.reshape(seq_len, H, E).transpose(1, 0, 2)

def join_heads(array, seq_len):
    return array.transpose(1, 0, 2).reshape(seq_len, H * E)

def reference(query, key, value, grad_out, neighbour, counts):
    seq_len = query.shape[0]

    def per_head(stacked):
        query_h, key_h, value_h, grad_h = stacked
        key_blocks = key_h.reshape(NB, BLK, E)
        value_blocks = value_h.reshape(NB, BLK, E)

        def per_shard(totals, inputs):
            query_g, grad_g, chosen, used = inputs
            usable = jnp.arange(NNB)[None, :] < used[:, None]
            out_g, dq_g, dk_part, dv_part = attend_blocks(query_g, grad_g, key_blocks[chosen], value_blocks[chosen], usable)
            flat = chosen.reshape(-1)
            key_total = totals[0].at[flat].add(dk_part.reshape(-1, BLK, E))
            value_total = totals[1].at[flat].add(dv_part.reshape(-1, BLK, E))
            return ((key_total, value_total), (out_g, dq_g))
        zeros_init = jnp.zeros((NB, BLK, E), jnp.float32)
        inputs = (query_h.reshape(N_CTX, BPS, BLK, E), grad_h.reshape(N_CTX, BPS, BLK, E), neighbour.reshape(N_CTX, BPS, NNB).astype(jnp.int32), counts.reshape(N_CTX, BPS).astype(jnp.int32))
        totals, results = lax.scan(per_shard, (zeros_init, zeros_init), inputs)
        return (results[0].reshape(seq_len, E), results[1].reshape(seq_len, E), totals[0].astype(jnp.bfloat16).reshape(seq_len, E), totals[1].astype(jnp.bfloat16).reshape(seq_len, E))
    results = lax.map(per_head, (split_heads(query, seq_len), split_heads(key, seq_len), split_heads(value, seq_len), split_heads(grad_out, seq_len)))
    return (join_heads(results[0], seq_len), join_heads(results[1], seq_len), join_heads(results[2], seq_len), join_heads(results[3], seq_len))
```

```python
import math

import jax
import jax.numpy as jnp
from jax import lax
from jax.experimental import pallas as pl
from jax.experimental.pallas import tpu as pltpu
from jax.sharding import Mesh, PartitionSpec as P

H = 16
E = 64
BLK = 128
NNB = 8
PLANES = 3
LOG2E = 1.4426950408889634

AXES = ("z", "yl", "yh", "x", "core")
HEADS = ("yl", "yh", "x")
VMEM = pltpu.VMEM


def pack_kernel(a_ref, b_ref, o_ref):
    for pair in range(H // 2):
        cols = slice(pair * 2 * E, (pair + 1) * 2 * E)
        a = a_ref[:, cols]
        b = b_ref[:, cols]
        o_ref[2 * pair] = jnp.concatenate([a[:, :E], b[:, :E]], axis=1)
        o_ref[2 * pair + 1] = jnp.concatenate([a[:, E:], b[:, E:]], axis=1)


def pack(a, b):
    rows = a.shape[0]
    return pl.pallas_call(
        pack_kernel,
        out_shape=jax.ShapeDtypeStruct((H, rows, 2 * E), a.dtype),
        in_specs=[pl.BlockSpec(memory_space=VMEM)] * 2,
        out_specs=pl.BlockSpec(memory_space=VMEM),
        name="pack",
    )(a, b)


def unpack_kernel(i_ref, a_ref, b_ref):
    for pair in range(H // 2):
        cols = slice(pair * 2 * E, (pair + 1) * 2 * E)
        even = i_ref[2 * pair]
        odd = i_ref[2 * pair + 1]
        a_ref[:, cols] = jnp.concatenate([even[:, :E], odd[:, :E]], axis=1)
        b_ref[:, cols] = jnp.concatenate([even[:, E:], odd[:, E:]], axis=1)


def unpack(joined):
    rows = joined.shape[1]
    shape = jax.ShapeDtypeStruct((rows, H * E), joined.dtype)
    return pl.pallas_call(
        unpack_kernel,
        out_shape=(shape, shape),
        in_specs=[pl.BlockSpec(memory_space=VMEM)],
        out_specs=[pl.BlockSpec(memory_space=VMEM)] * 2,
        name="unpack",
    )(joined)


def attend_block(s, slots, used, index_of, qg_ref, win, acc, st, oq_ref):
    qg = qg_ref[s]
    low = lax.broadcasted_iota(jnp.int32, (BLK, 2 * E), 1) < E
    zero = jnp.zeros_like(qg)
    both = jnp.concatenate(
        [jnp.where(low, qg * jnp.bfloat16(0.125), zero), jnp.where(low, zero, qg)], axis=0
    )
    where = [index_of(j) for j in range(slots)]
    highest = None
    for j in range(slots):
        pair = lax.dot_general(
            win[where[j]], both, (((1,), (1,)), ((), ())), preferred_element_type=jnp.float32
        )
        scores = pair[:, :BLK]
        if j == slots - 1:
            scores = jnp.where(j < used, scores, -1e30)
        st[j, :, :BLK] = scores
        st[j, :, BLK:] = pair[:, BLK:]
        top = jnp.max(scores, axis=0, keepdims=True)
        highest = top if highest is None else jnp.maximum(highest, top)
    total = jnp.zeros((1, BLK), jnp.float32)
    mixed = jnp.zeros((1, BLK), jnp.float32)
    for j in range(slots):
        raised = jnp.exp2((st[j, :, :BLK] - highest) * LOG2E)
        st[j, :, :BLK] = raised
        total = total + jnp.sum(raised, axis=0, keepdims=True)
        mixed = mixed + jnp.sum(raised * st[j, :, BLK:], axis=0, keepdims=True)
    inverse = 1.0 / total
    delta = mixed * inverse
    sums = None
    for j in range(slots):
        probability = st[j, :, :BLK] * inverse
        dscore = probability * (st[j, :, BLK:] - delta)
        joined = jnp.concatenate(
            [dscore.astype(jnp.bfloat16), probability.astype(jnp.bfloat16)], axis=1
        )
        acc[where[j]] += jnp.dot(joined, both, preferred_element_type=jnp.float32)
        part = jnp.dot(win[where[j]].T, joined, preferred_element_type=jnp.float32)
        sums = part if sums is None else sums + part
    result = jnp.concatenate([sums[:E, :BLK] * 0.125, sums[E:, BLK:]], axis=0)
    oq_ref[s] = result.T.astype(oq_ref.dtype)


def attend_kernel(
    place, variants, nbr, cnt, qg_ref, *rest
):
    kv_refs = rest[:6]
    oq_ref, own_ref, other_ref = rest[6:9]
    win, acc, st, sems = rest[9:]
    z, core = place()
    blocks = qg_ref.shape[0]
    plane_blocks = 2 * blocks
    all_blocks = cnt.shape[0]
    copies = [
        pltpu.make_async_copy(kv_refs[i], win.at[pl.ds(i * blocks, blocks)], sems.at[i])
        for i in range(6)
    ]
    for copy in copies:
        copy.start()
    first = (z - 1) * plane_blocks

    @pl.loop(0, 6 * blocks)
    def _(i):
        acc[i] = jnp.zeros_like(acc[i])

    for copy in copies:
        copy.wait()

    @pl.loop(0, blocks)
    def _(s):
        b = z * plane_blocks + 2 * s + core
        used = cnt[b]

        def index_of(j):
            rel = lax.rem(nbr[j, b] - first + all_blocks, all_blocks)
            side = lax.rem(rel + core, 2)
            return side * (PLANES * blocks) + lax.div(rel, 2)

        before = 0
        for slots in variants:

            @pl.when((used > before) & (used <= slots))
            def _(slots=slots):
                attend_block(s, slots, used, index_of, qg_ref, win, acc, st, oq_ref)

            before = slots

    own_ref[...] = acc[pl.ds(0, PLANES * blocks)]

    @pl.loop(0, PLANES * blocks)
    def _(i):
        other_ref[i] = acc[PLANES * blocks + i].astype(other_ref.dtype)


def attend(place, nbr_t, counts, qg, kvs, variants=(2, 4, 6, 8)):
    import functools

    blocks = qg.shape[0]
    tile = (BLK, 2 * E)
    return pl.pallas_call(
        functools.partial(attend_kernel, place, variants),
        out_shape=(
            jax.ShapeDtypeStruct((blocks,) + tile, jnp.bfloat16),
            jax.ShapeDtypeStruct((PLANES * blocks,) + tile, jnp.float32),
            jax.ShapeDtypeStruct((PLANES * blocks,) + tile, jnp.bfloat16),
        ),
        in_specs=[pl.BlockSpec(memory_space=pltpu.SMEM)] * 2
        + [pl.BlockSpec(memory_space=VMEM)]
        + [pl.BlockSpec(memory_space=pl.ANY)] * 6,
        out_specs=[pl.BlockSpec(memory_space=VMEM)] * 3,
        scratch_shapes=[
            pltpu.VMEM((6 * blocks,) + tile, jnp.bfloat16),
            pltpu.VMEM((6 * blocks,) + tile, jnp.float32),
            pltpu.VMEM((NNB, BLK, 2 * BLK), jnp.float32),
            pltpu.SemaphoreType.DMA((6,)),
        ],
        compiler_params=pltpu.CompilerParams(vmem_limit_bytes=40 << 20),
        cost_estimate=pl.CostEstimate(
            flops=2 * 5 * blocks * 5 * BLK * BLK * E,
            bytes_accessed=8 << 20,
            transcendentals=blocks * 5 * BLK * BLK,
        ),
        name="attend",
    )(nbr_t, counts, qg, *kvs)


def on_device(query, key, value, grad_out, neighbour, counts):
    planes = lax.axis_size("z")
    up = [(i, (i + 1) % planes) for i in range(planes)]
    down = [(i, (i - 1) % planes) for i in range(planes)]
    swap = [(0, 1), (1, 0)]

    def exchange(packed):
        return lax.all_to_all(packed, HEADS, split_axis=0, concat_axis=0, tiled=True)

    kv = exchange(pack(key, value))
    kv_before = lax.ppermute(kv, "z", up)
    kv_after = lax.ppermute(kv, "z", down)
    qg = exchange(pack(query, grad_out))
    kv_other = lax.ppermute(kv, "core", swap)
    before_other = lax.ppermute(kv_before, "core", swap)
    after_other = lax.ppermute(kv_after, "core", swap)

    def place():
        return lax.axis_index("z"), lax.axis_index("core")

    oq, own, other = attend(
        place,
        neighbour.T,
        counts,
        qg,
        (kv_before, kv, kv_after, before_other, kv_other, after_other),
    )
    blocks = qg.shape[0]
    mine = lax.ppermute(other, "core", swap)
    sums = own + mine.astype(jnp.float32)
    to_before = sums[:blocks].astype(jnp.bfloat16)
    to_after = sums[2 * blocks :].astype(jnp.bfloat16)
    from_after = lax.ppermute(to_before, "z", down)
    from_before = lax.ppermute(to_after, "z", up)
    back_oq = exchange(oq)
    total = (
        sums[blocks : 2 * blocks]
        + from_after.astype(jnp.float32)
        + from_before.astype(jnp.float32)
    ).astype(jnp.bfloat16)
    dquery, out = unpack(back_oq)
    dkey, dvalue = unpack(exchange(total))
    return out, dquery, dkey, dvalue


def solution(mesh):
    inner = Mesh(mesh.devices.reshape(16, 2, 2, 4, 2), AXES)
    return jax.shard_map(
        on_device,
        mesh=inner,
        in_specs=(P(AXES, None),) * 4 + (P(), P()),
        out_specs=(P(AXES, None),) * 4,
        check_vma=False,
    )
```

```python
import math

import jax
import jax.numpy as jnp
from jax import lax
from jax.experimental import pallas as pl
from jax.experimental.pallas import tpu as pltpu
from jax.sharding import Mesh, PartitionSpec as P

H = 16
E = 64
BLK = 128
NNB = 8
PLANES = 3
PACK_STEPS = 4
LOG2E = 1.4426950408889634

AXES = ("z", "yl", "yh", "x", "core")
HEADS = ("yl", "yh", "x")
VMEM = pltpu.VMEM


def pack_kernel(a_hbm, b_hbm, o_hbm, a_buf, b_buf, o_buf, in_sems, out_sems):
    wide = 2 * E * H // 2 // PACK_STEPS
    tall = H // PACK_STEPS

    def fetch(src, dst, which, i):
        cols = pl.ds(i * wide, wide)
        return pltpu.make_async_copy(src.at[:, cols], dst.at[:, cols], in_sems.at[which, i])

    def put(i):
        rows = pl.ds(i * tall, tall)
        return pltpu.make_async_copy(o_buf.at[rows], o_hbm.at[rows], out_sems.at[i])

    for i in range(PACK_STEPS):
        fetch(a_hbm, a_buf, 0, i).start()
        fetch(b_hbm, b_buf, 1, i).start()
    for i in range(PACK_STEPS):
        fetch(a_hbm, a_buf, 0, i).wait()
        fetch(b_hbm, b_buf, 1, i).wait()
        for pair in range(i * tall // 2, (i + 1) * tall // 2):
            cols = slice(pair * 2 * E, (pair + 1) * 2 * E)
            a = a_buf[:, cols]
            b = b_buf[:, cols]
            o_buf[2 * pair] = jnp.concatenate([a[:, :E], b[:, :E]], axis=1)
            o_buf[2 * pair + 1] = jnp.concatenate([a[:, E:], b[:, E:]], axis=1)
        put(i).start()
    for i in range(PACK_STEPS):
        put(i).wait()


def pack(a, b):
    rows, width = a.shape
    joined = (H, rows, 2 * E)
    return pl.pallas_call(
        pack_kernel,
        out_shape=jax.ShapeDtypeStruct(joined, a.dtype),
        in_specs=[pl.BlockSpec(memory_space=pl.ANY)] * 2,
        out_specs=pl.BlockSpec(memory_space=pl.ANY),
        scratch_shapes=[
            pltpu.VMEM((rows, width), a.dtype),
            pltpu.VMEM((rows, width), a.dtype),
            pltpu.VMEM(joined, a.dtype),
            pltpu.SemaphoreType.DMA((2, PACK_STEPS)),
            pltpu.SemaphoreType.DMA((PACK_STEPS,)),
        ],
        cost_estimate=pl.CostEstimate(flops=0, bytes_accessed=1 << 20, transcendentals=0),
        name="pack",
    )(a, b)


def unpack_kernel(i_ref, a_ref, b_ref):
    for pair in range(H // 2):
        cols = slice(pair * 2 * E, (pair + 1) * 2 * E)
        even = i_ref[2 * pair]
        odd = i_ref[2 * pair + 1]
        a_ref[:, cols] = jnp.concatenate([even[:, :E], odd[:, :E]], axis=1)
        b_ref[:, cols] = jnp.concatenate([even[:, E:], odd[:, E:]], axis=1)


def unpack(joined):
    rows = joined.shape[1]
    shape = jax.ShapeDtypeStruct((rows, H * E), joined.dtype)
    return pl.pallas_call(
        unpack_kernel,
        out_shape=(shape, shape),
        in_specs=[pl.BlockSpec(memory_space=VMEM)],
        out_specs=[pl.BlockSpec(memory_space=VMEM)] * 2,
        compiler_params=pltpu.CompilerParams(vmem_limit_bytes=4 << 20),
        cost_estimate=pl.CostEstimate(flops=0, bytes_accessed=1 << 20, transcendentals=0),
        name="unpack",
    )(joined)


def sides_kernel(own_ref, mine_ref, before_ref, after_ref, here_ref):
    blocks = before_ref.shape[0]

    @pl.loop(0, blocks)
    def _(i):
        before = own_ref[i] + mine_ref[i].astype(jnp.float32)
        after = own_ref[2 * blocks + i] + mine_ref[2 * blocks + i].astype(jnp.float32)
        before_ref[i] = before.astype(before_ref.dtype)
        after_ref[i] = after.astype(after_ref.dtype)
        here_ref[i] = own_ref[blocks + i] + mine_ref[blocks + i].astype(jnp.float32)


def sides(own, mine):
    shape = jax.ShapeDtypeStruct((own.shape[0] // PLANES,) + own.shape[1:], mine.dtype)
    return pl.pallas_call(
        sides_kernel,
        out_shape=(shape, shape, jax.ShapeDtypeStruct(shape.shape, jnp.float32)),
        in_specs=[pl.BlockSpec(memory_space=VMEM)] * 2,
        out_specs=[pl.BlockSpec(memory_space=VMEM)] * 3,
        compiler_params=pltpu.CompilerParams(vmem_limit_bytes=8 << 20),
        cost_estimate=pl.CostEstimate(flops=0, bytes_accessed=4 << 20, transcendentals=0),
        name="sides",
    )(own, mine)


def finish_kernel(here_ref, first_ref, second_ref, o_hbm, o_buf, sems):
    blocks = here_ref.shape[0]
    tall = blocks // PACK_STEPS

    def put(i):
        rows = pl.ds(i * tall, tall)
        return pltpu.make_async_copy(o_buf.at[rows], o_hbm.at[rows], sems.at[i])

    for i in range(PACK_STEPS):
        for j in range(i * tall, (i + 1) * tall):
            total = first_ref[j].astype(jnp.float32) + second_ref[j].astype(jnp.float32)
            total = here_ref[j] + total
            o_buf[j] = total.astype(o_buf.dtype)
        put(i).start()
    for i in range(PACK_STEPS):
        put(i).wait()


def finish(here, first, second):
    return pl.pallas_call(
        finish_kernel,
        out_shape=jax.ShapeDtypeStruct(first.shape, first.dtype),
        in_specs=[pl.BlockSpec(memory_space=VMEM)] * 3,
        out_specs=pl.BlockSpec(memory_space=pl.ANY),
        scratch_shapes=[pltpu.VMEM(first.shape, first.dtype), pltpu.SemaphoreType.DMA((PACK_STEPS,))],
        compiler_params=pltpu.CompilerParams(vmem_limit_bytes=8 << 20),
        cost_estimate=pl.CostEstimate(flops=0, bytes_accessed=3 << 20, transcendentals=0),
        name="finish",
    )(here, first, second)


def attend_group(group, slots, index_of, qg_ref, win, acc, st, oq_ref):
    low = lax.broadcasted_iota(jnp.int32, (BLK, 2 * E), 1) < E
    members = range(len(group))
    both = []
    where = []
    for s, b, used in group:
        qg = qg_ref[s]
        zero = jnp.zeros_like(qg)
        both.append(
            jnp.concatenate(
                [jnp.where(low, qg * jnp.bfloat16(0.125), zero), jnp.where(low, zero, qg)], axis=0
            )
        )
        where.append([index_of(j, b) for j in range(slots)])
    highest = [None for _ in members]
    for j in range(slots):
        for m in members:
            pair = lax.dot_general(
                win[where[m][j]],
                both[m],
                (((1,), (1,)), ((), ())),
                preferred_element_type=jnp.float32,
            )
            scores = pair[:, :BLK]
            if j > 0:
                scores = jnp.where(j < group[m][2], scores, -1e30)
            st[m, j, :, :BLK] = scores
            st[m, j, :, BLK:] = pair[:, BLK:]
            top = jnp.max(scores, axis=0, keepdims=True)
            highest[m] = top if j == 0 else jnp.maximum(highest[m], top)
    total = [jnp.zeros((1, BLK), jnp.float32) for _ in members]
    mixed = [jnp.zeros((1, BLK), jnp.float32) for _ in members]
    for j in range(slots):
        for m in members:
            raised = jnp.exp2((st[m, j, :, :BLK] - highest[m]) * LOG2E)
            st[m, j, :, :BLK] = raised
            total[m] = total[m] + jnp.sum(raised, axis=0, keepdims=True)
            mixed[m] = mixed[m] + jnp.sum(raised * st[m, j, :, BLK:], axis=0, keepdims=True)
    inverse = [1.0 / total[m] for m in members]
    delta = [mixed[m] * inverse[m] for m in members]
    sums = [None for _ in members]
    for j in range(slots):
        for m in members:
            probability = st[m, j, :, :BLK] * inverse[m]
            dscore = probability * (st[m, j, :, BLK:] - delta[m])
            joined = jnp.concatenate(
                [dscore.astype(jnp.bfloat16), probability.astype(jnp.bfloat16)], axis=1
            )
            acc[where[m][j]] += jnp.dot(joined, both[m], preferred_element_type=jnp.float32)
            part = jnp.dot(win[where[m][j]].T, joined, preferred_element_type=jnp.float32)
            sums[m] = part if j == 0 else sums[m] + part
    for m in members:
        result = jnp.concatenate([sums[m][:E, :BLK] * 0.125, sums[m][E:, BLK:]], axis=0)
        oq_ref[group[m][0]] = result.T.astype(oq_ref.dtype)


def attend_kernel(
    place, variants, size, nbr, cnt, qg_ref, *rest
):
    kv_refs = rest[:6]
    oq_ref, own_ref, other_ref = rest[6:9]
    win, acc, st, order, fill, sems = rest[9:]
    z, core = place()
    blocks = qg_ref.shape[0]
    plane_blocks = 2 * blocks
    all_blocks = cnt.shape[0]
    copies = [
        pltpu.make_async_copy(kv_refs[i], win.at[pl.ds(i * blocks, blocks)], sems.at[i])
        for i in range(6)
    ]
    for copy in copies:
        copy.start()
    first = (z - 1) * plane_blocks

    @pl.loop(0, 6 * blocks)
    def _(i):
        acc[i] = jnp.zeros_like(acc[i])

    def block_of(s):
        return z * plane_blocks + 2 * s + core

    for c in range(NNB + 2):
        fill[c] = 0

    @pl.loop(0, blocks)
    def _(s):
        c = cnt[block_of(s)]
        fill[c + 1] += 1

    for c in range(2, NNB + 1):
        fill[c] += fill[c - 1]

    @pl.loop(0, blocks)
    def _(s):
        c = cnt[block_of(s)]
        order[fill[c]] = s
        fill[c] += 1

    for copy in copies:
        copy.wait()

    def index_of(j, b):
        rel = lax.rem(nbr[j, b] - first + all_blocks, all_blocks)
        side = lax.rem(rel + core, 2)
        return side * (PLANES * blocks) + lax.div(rel, 2)

    @pl.loop(0, blocks // size)
    def _(i):
        group = []
        for m in range(size):
            s = order[i * size + m]
            b = block_of(s)
            group.append((s, b, cnt[b]))
        most = group[-1][2]
        before = 0
        for slots in variants:

            @pl.when((most > before) & (most <= slots))
            def _(slots=slots):
                attend_group(group, slots, index_of, qg_ref, win, acc, st, oq_ref)

            before = slots

    @pl.loop(0, PLANES * blocks)
    def _(i):
        own_ref[i] = acc[i]
        other_ref[i] = acc[PLANES * blocks + i].astype(other_ref.dtype)


def attend(place, nbr_t, counts, qg, kvs, variants=(2, 4, 6, 8), size=4):
    import functools

    blocks = qg.shape[0]
    tile = (BLK, 2 * E)
    return pl.pallas_call(
        functools.partial(attend_kernel, place, variants, size),
        out_shape=(
            jax.ShapeDtypeStruct((blocks,) + tile, jnp.bfloat16),
            jax.ShapeDtypeStruct((PLANES * blocks,) + tile, jnp.float32),
            jax.ShapeDtypeStruct((PLANES * blocks,) + tile, jnp.bfloat16),
        ),
        in_specs=[pl.BlockSpec(memory_space=pltpu.SMEM)] * 2
        + [pl.BlockSpec(memory_space=VMEM)]
        + [pl.BlockSpec(memory_space=pltpu.HBM)] * 6,
        out_specs=[pl.BlockSpec(memory_space=VMEM)] * 3,
        scratch_shapes=[
            pltpu.VMEM((6 * blocks,) + tile, jnp.bfloat16),
            pltpu.VMEM((6 * blocks,) + tile, jnp.float32),
            pltpu.VMEM((size, NNB, BLK, 2 * BLK), jnp.float32),
            pltpu.SMEM((blocks,), jnp.int32),
            pltpu.SMEM((NNB + 2,), jnp.int32),
            pltpu.SemaphoreType.DMA((6,)),
        ],
        compiler_params=pltpu.CompilerParams(vmem_limit_bytes=18 << 20),
        cost_estimate=pl.CostEstimate(
            flops=2 * 5 * blocks * 5 * BLK * BLK * E,
            bytes_accessed=8 << 20,
            transcendentals=blocks * 5 * BLK * BLK,
        ),
        name="attend",
    )(nbr_t, counts, qg, *kvs)


def on_device(query, key, value, grad_out, neighbour, counts):
    planes = lax.axis_size("z")
    up = [(i, (i + 1) % planes) for i in range(planes)]
    down = [(i, (i - 1) % planes) for i in range(planes)]
    swap = [(0, 1), (1, 0)]

    def exchange(packed):
        return lax.all_to_all(packed, HEADS, split_axis=0, concat_axis=0, tiled=True)

    kv = exchange(pack(key, value))
    kv, qg_packed = lax.optimization_barrier((kv, pack(query, grad_out)))
    kv_before = lax.ppermute(kv, "z", up)
    kv_after = lax.ppermute(kv, "z", down)
    qg = exchange(qg_packed)
    kv_other = lax.ppermute(kv, "core", swap)
    kv_before, kv_after, qg = lax.optimization_barrier((kv_before, kv_after, qg))
    before_other = lax.ppermute(kv_before, "core", swap)
    after_other = lax.ppermute(kv_after, "core", swap)

    def place():
        return lax.axis_index("z"), lax.axis_index("core")

    oq, own, other = attend(
        place,
        neighbour.T,
        counts,
        qg,
        (kv_before, kv, kv_after, before_other, kv_other, after_other),
    )
    mine = lax.ppermute(other, "core", swap)
    to_before, to_after, here = sides(own, mine)
    from_after = lax.ppermute(to_before, "z", down)
    from_before = lax.ppermute(to_after, "z", up)
    back_oq = exchange(oq)
    total = finish(here, from_after, from_before)
    dquery, out = unpack(back_oq)
    dkey, dvalue = unpack(exchange(total))
    return out, dquery, dkey, dvalue


def solution(mesh):
    inner = Mesh(mesh.devices.reshape(16, 2, 2, 4, 2), AXES)
    return jax.shard_map(
        on_device,
        mesh=inner,
        in_specs=(P(AXES, None),) * 4 + (P(), P()),
        out_specs=(P(AXES, None),) * 4,
        check_vma=False,
    )
```

```python
import functools

import jax
import jax.numpy as jnp
from jax import lax
from jax.experimental import pallas as pl
from jax.experimental.pallas import tpu as pltpu
from jax.sharding import Mesh, PartitionSpec as P

H = 16
E = 64
BLK = 128
NNB = 8
PLANES = 3
PACK_STEPS = 4
LOG2E = 1.4426950408889634

AXES = ("z", "yl", "yh", "x", "core")
HEADS = ("yl", "yh", "x")
VMEM = pltpu.VMEM


def pack_kernel(a_hbm, b_hbm, o_hbm, a_buf, b_buf, o_buf, in_sems, out_sems):
    wide = 2 * E * H // 2 // PACK_STEPS
    tall = H // PACK_STEPS

    def fetch(src, dst, which, i):
        cols = pl.ds(i * wide, wide)
        return pltpu.make_async_copy(src.at[:, cols], dst.at[:, cols], in_sems.at[which, i])

    def put(i):
        rows = pl.ds(i * tall, tall)
        return pltpu.make_async_copy(o_buf.at[rows], o_hbm.at[rows], out_sems.at[i])

    for i in range(PACK_STEPS):
        fetch(a_hbm, a_buf, 0, i).start()
        fetch(b_hbm, b_buf, 1, i).start()
    for i in range(PACK_STEPS):
        fetch(a_hbm, a_buf, 0, i).wait()
        fetch(b_hbm, b_buf, 1, i).wait()
        for pair in range(i * tall // 2, (i + 1) * tall // 2):
            cols = slice(pair * 2 * E, (pair + 1) * 2 * E)
            a = a_buf[:, cols]
            b = b_buf[:, cols]
            o_buf[2 * pair] = jnp.concatenate([a[:, :E], b[:, :E]], axis=1)
            o_buf[2 * pair + 1] = jnp.concatenate([a[:, E:], b[:, E:]], axis=1)
        put(i).start()
    for i in range(PACK_STEPS):
        put(i).wait()


def pack(a, b):
    rows, width = a.shape
    joined = (H, rows, 2 * E)
    return pl.pallas_call(
        pack_kernel,
        out_shape=jax.ShapeDtypeStruct(joined, a.dtype),
        in_specs=[pl.BlockSpec(memory_space=pl.ANY)] * 2,
        out_specs=pl.BlockSpec(memory_space=pl.ANY),
        scratch_shapes=[
            pltpu.VMEM((rows, width), a.dtype),
            pltpu.VMEM((rows, width), a.dtype),
            pltpu.VMEM(joined, a.dtype),
            pltpu.SemaphoreType.DMA((2, PACK_STEPS)),
            pltpu.SemaphoreType.DMA((PACK_STEPS,)),
        ],
        cost_estimate=pl.CostEstimate(flops=0, bytes_accessed=1 << 20, transcendentals=0),
        name="pack",
    )(a, b)


def unpack_kernel(i_ref, a_ref, b_ref):
    for pair in range(H // 2):
        cols = slice(pair * 2 * E, (pair + 1) * 2 * E)
        even = i_ref[2 * pair]
        odd = i_ref[2 * pair + 1]
        a_ref[:, cols] = jnp.concatenate([even[:, :E], odd[:, :E]], axis=1)
        b_ref[:, cols] = jnp.concatenate([even[:, E:], odd[:, E:]], axis=1)


def unpack(joined):
    rows = joined.shape[1]
    shape = jax.ShapeDtypeStruct((rows, H * E), joined.dtype)
    return pl.pallas_call(
        unpack_kernel,
        out_shape=(shape, shape),
        in_specs=[pl.BlockSpec(memory_space=VMEM)],
        out_specs=[pl.BlockSpec(memory_space=VMEM)] * 2,
        compiler_params=pltpu.CompilerParams(vmem_limit_bytes=4 << 20),
        cost_estimate=pl.CostEstimate(flops=0, bytes_accessed=1 << 20, transcendentals=0),
        name="unpack",
    )(joined)


def sides_kernel(own_ref, mine_ref, before_ref, after_ref, here_ref):
    blocks = before_ref.shape[0]

    @pl.loop(0, blocks)
    def _(i):
        before = own_ref[i] + mine_ref[i].astype(jnp.float32)
        after = own_ref[2 * blocks + i] + mine_ref[2 * blocks + i].astype(jnp.float32)
        before_ref[i] = before.astype(before_ref.dtype)
        after_ref[i] = after.astype(after_ref.dtype)
        here_ref[i] = own_ref[blocks + i] + mine_ref[blocks + i].astype(jnp.float32)


def sides(own, mine):
    shape = jax.ShapeDtypeStruct((own.shape[0] // PLANES,) + own.shape[1:], mine.dtype)
    return pl.pallas_call(
        sides_kernel,
        out_shape=(shape, shape, jax.ShapeDtypeStruct(shape.shape, jnp.float32)),
        in_specs=[pl.BlockSpec(memory_space=VMEM)] * 2,
        out_specs=[pl.BlockSpec(memory_space=VMEM)] * 3,
        compiler_params=pltpu.CompilerParams(vmem_limit_bytes=8 << 20),
        cost_estimate=pl.CostEstimate(flops=0, bytes_accessed=4 << 20, transcendentals=0),
        name="sides",
    )(own, mine)


def finish_kernel(here_ref, first_ref, second_ref, o_hbm, o_buf, sems):
    blocks = here_ref.shape[0]
    tall = blocks // PACK_STEPS

    def put(i):
        rows = pl.ds(i * tall, tall)
        return pltpu.make_async_copy(o_buf.at[rows], o_hbm.at[rows], sems.at[i])

    for i in range(PACK_STEPS):
        for j in range(i * tall, (i + 1) * tall):
            total = first_ref[j].astype(jnp.float32) + second_ref[j].astype(jnp.float32)
            total = here_ref[j] + total
            o_buf[j] = total.astype(o_buf.dtype)
        put(i).start()
    for i in range(PACK_STEPS):
        put(i).wait()


def finish(here, first, second):
    return pl.pallas_call(
        finish_kernel,
        out_shape=jax.ShapeDtypeStruct(first.shape, first.dtype),
        in_specs=[pl.BlockSpec(memory_space=VMEM)] * 3,
        out_specs=pl.BlockSpec(memory_space=pl.ANY),
        scratch_shapes=[pltpu.VMEM(first.shape, first.dtype), pltpu.SemaphoreType.DMA((PACK_STEPS,))],
        compiler_params=pltpu.CompilerParams(vmem_limit_bytes=8 << 20),
        cost_estimate=pl.CostEstimate(flops=0, bytes_accessed=3 << 20, transcendentals=0),
        name="finish",
    )(here, first, second)


def plan_kernel(place, nbr, cnt, plan, fill):
    z, core = place()
    blocks = plan.shape[0]
    plane_blocks = 2 * blocks
    all_blocks = cnt.shape[0]
    first = (z - 1) * plane_blocks

    def block_of(s):
        return z * plane_blocks + 2 * s + core

    for c in range(NNB + 2):
        fill[c] = 0

    @pl.loop(0, blocks)
    def _(s):
        c = cnt[block_of(s)]
        fill[c + 1] += 1

    for c in range(2, NNB + 1):
        fill[c] += fill[c - 1]

    @pl.loop(0, blocks)
    def _(s):
        b = block_of(s)
        c = cnt[b]
        at = fill[c]
        fill[c] += 1
        plan[at, NNB] = s
        plan[at, NNB + 1] = c
        for j in range(NNB):
            rel = lax.rem(nbr[j, b] - first + all_blocks, all_blocks)
            side = lax.rem(rel + core, 2)
            plane = lax.div(rel, plane_blocks)
            slot = jnp.where(lax.rem(rel, 2) == 1, PLANES - 1 - plane, plane)
            plan[at, j] = (side * PLANES + slot) * blocks + lax.div(
                lax.rem(rel, plane_blocks), 2
            )


def plan_blocks(place, nbr_t, counts, blocks):
    return pl.pallas_call(
        functools.partial(plan_kernel, place),
        out_shape=jax.ShapeDtypeStruct((blocks, 2 * NNB), jnp.int32),
        in_specs=[pl.BlockSpec(memory_space=pltpu.SMEM)] * 2,
        out_specs=pl.BlockSpec(memory_space=pltpu.SMEM),
        scratch_shapes=[pltpu.SMEM((NNB + 2,), jnp.int32)],
        compiler_params=pltpu.CompilerParams(vmem_limit_bytes=1 << 20),
        cost_estimate=pl.CostEstimate(flops=0, bytes_accessed=1 << 20, transcendentals=0),
        name="plan",
    )(nbr_t, counts)


def join_kernel(a_ref, b_ref, o_ref):
    blocks = a_ref.shape[0]
    o_ref[:blocks] = a_ref[...]
    o_ref[blocks:] = b_ref[...]


def join(a, b):
    return pl.pallas_call(
        join_kernel,
        out_shape=jax.ShapeDtypeStruct((2 * a.shape[0],) + a.shape[1:], a.dtype),
        in_specs=[pl.BlockSpec(memory_space=VMEM)] * 2,
        out_specs=pl.BlockSpec(memory_space=VMEM),
        compiler_params=pltpu.CompilerParams(vmem_limit_bytes=4 << 20),
        cost_estimate=pl.CostEstimate(flops=0, bytes_accessed=2 << 20, transcendentals=0),
        name="join",
    )(a, b)


def attend_group(group, slots, qg_ref, win, acc, st, jn, oq_ref):
    low = lax.broadcasted_iota(jnp.int32, (BLK, 2 * E), 1) < E
    members = range(len(group))
    both = []
    where = []
    for s, used, found in group:
        qg = qg_ref[s]
        zero = jnp.zeros_like(qg)
        both.append(
            jnp.concatenate(
                [jnp.where(low, qg * jnp.bfloat16(0.125), zero), jnp.where(low, zero, qg)], axis=0
            )
        )
        where.append([found(j) for j in range(slots)])
    rows = [slice(j * BLK, (j + 1) * BLK) for j in range(slots)]
    everything = slice(0, slots * BLK)
    live = [[j == 0 or j < used for j in range(slots)] for _, used, _ in group]
    tops = []
    for m in members:
        keys = jnp.concatenate([win[where[m][j]] for j in range(slots)], axis=0)
        st[m, everything] = lax.dot_general(
            keys, both[m], (((1,), (1,)), ((), ())), preferred_element_type=jnp.float32
        )
        top = [jnp.max(st[m, rows[j], :BLK], axis=0, keepdims=True) for j in range(slots)]
        highest = top[0]
        for j in range(1, slots):
            highest = jnp.maximum(highest, jnp.where(live[m][j], top[j], -1e30))
        tops.append(
            [highest if j == 0 else jnp.where(live[m][j], highest, 1e30) for j in range(slots)]
        )
    inverse = []
    delta = []
    for m in members:
        total = jnp.zeros((1, BLK), jnp.float32)
        mixed = jnp.zeros((1, BLK), jnp.float32)
        for j in range(slots):
            raised = jnp.exp2((st[m, rows[j], :BLK] - tops[m][j]) * LOG2E)
            st[m, rows[j], :BLK] = raised
            total = total + jnp.sum(raised, axis=0, keepdims=True)
            mixed = mixed + jnp.sum(raised * st[m, rows[j], BLK:], axis=0, keepdims=True)
        inverse.append(1.0 / total)
        delta.append(mixed * inverse[m])
    for m in members:
        for j in range(slots):
            probability = st[m, rows[j], :BLK] * inverse[m]
            dscore = probability * (st[m, rows[j], BLK:] - delta[m])
            jn[m, rows[j], :BLK] = dscore.astype(jnp.bfloat16)
            jn[m, rows[j], BLK:] = probability.astype(jnp.bfloat16)
        joined = jn[m, everything]
        parts = jnp.dot(joined, both[m], preferred_element_type=jnp.float32)
        for j in range(slots):
            acc[where[m][j]] += parts[rows[j]]
        turned = jnp.concatenate([win[where[m][j]].T for j in range(slots)], axis=1)
        sums = jnp.dot(turned, joined, preferred_element_type=jnp.float32)
        result = jnp.concatenate([sums[:E, :BLK] * 0.125, sums[E:, BLK:]], axis=0)
        oq_ref[group[m][0]] = result.T.astype(oq_ref.dtype)


def entry(plan, at, j):
    return plan[at, j]


def attend_kernel(variants, size, plan, qg_ref, *rest):
    kv_refs = rest[:4]
    oq_ref, own_ref, other_ref = rest[4:7]
    win, acc, st, jn, sems = rest[7:]
    blocks = qg_ref.shape[0]
    pieces = (
        (1, 0, 0), (0, 0, 1), (2, 1, 1), (4, 0, 2), (3, 0, 3), (5, 1, 3)
    )
    copies = [
        pltpu.make_async_copy(
            kv_refs[which].at[pl.ds(part * blocks, blocks)],
            win.at[pl.ds(slot * blocks, blocks)],
            sems.at[slot],
        )
        for slot, part, which in pieces
    ]
    for copy in copies:
        copy.start()

    @pl.loop(0, 2 * PLANES * blocks)
    def _(i):
        acc[i] = jnp.zeros_like(acc[i])

    for copy in copies:
        copy.wait()

    @pl.loop(0, blocks // size)
    def _(i):
        group = []
        for m in range(size):
            at = i * size + m
            group.append((plan[at, NNB], plan[at, NNB + 1], functools.partial(entry, plan, at)))
        most = group[-1][1]
        before = 0
        for slots in variants:

            @pl.when((most > before) & (most <= slots))
            def _(slots=slots):
                attend_group(group, slots, qg_ref, win, acc, st, jn, oq_ref)

            before = slots

    @pl.loop(0, PLANES * blocks)
    def _(i):
        own_ref[i] = acc[i]
        other_ref[i] = acc[PLANES * blocks + i].astype(other_ref.dtype)


def attend(plan, qg, kvs, variants=(1, 2, 3, 4, 5, 6, 7, 8), size=4):
    blocks = qg.shape[0]
    tile = (BLK, 2 * E)
    return pl.pallas_call(
        functools.partial(attend_kernel, variants, size),
        out_shape=(
            jax.ShapeDtypeStruct((blocks,) + tile, jnp.bfloat16),
            jax.ShapeDtypeStruct((PLANES * blocks,) + tile, jnp.float32),
            jax.ShapeDtypeStruct((PLANES * blocks,) + tile, jnp.bfloat16),
        ),
        in_specs=[pl.BlockSpec(memory_space=pltpu.SMEM), pl.BlockSpec(memory_space=VMEM)]
        + [pl.BlockSpec(memory_space=pltpu.HBM)] * 4,
        out_specs=[pl.BlockSpec(memory_space=VMEM)] * 3,
        scratch_shapes=[
            pltpu.VMEM((6 * blocks,) + tile, jnp.bfloat16),
            pltpu.VMEM((6 * blocks,) + tile, jnp.float32),
            pltpu.VMEM((size, NNB * BLK, 2 * BLK), jnp.float32),
            pltpu.VMEM((size, NNB * BLK, 2 * BLK), jnp.bfloat16),
            pltpu.SemaphoreType.DMA((6,)),
        ],
        compiler_params=pltpu.CompilerParams(vmem_limit_bytes=32 << 20),
        cost_estimate=pl.CostEstimate(
            flops=2 * 5 * blocks * 5 * BLK * BLK * E,
            bytes_accessed=8 << 20,
            transcendentals=blocks * 5 * BLK * BLK,
        ),
        name="attend",
    )(plan, qg, *kvs)


def on_device(query, key, value, grad_out, neighbour, counts):
    planes = lax.axis_size("z")
    out_pairs = []
    in_pairs = []
    for i in range(planes):
        for core in range(2):
            ahead = (i + 1 - 2 * core) % planes
            out_pairs.append((2 * i + core, 2 * ahead + core))
            in_pairs.append((2 * ahead + core, 2 * i + core))
    swap = [(0, 1), (1, 0)]

    def place():
        return lax.axis_index("z"), lax.axis_index("core")

    def exchange(packed):
        return lax.all_to_all(packed, HEADS, split_axis=0, concat_axis=0, tiled=True)

    kv = exchange(pack(key, value))
    blocks = kv.shape[0]
    plan = plan_blocks(place, neighbour.T, counts, blocks)
    kv, qg_packed, plan = lax.optimization_barrier((kv, pack(query, grad_out), plan))
    kv_first = lax.ppermute(kv, ("z", "core"), out_pairs)
    kv_second = lax.ppermute(kv, ("z", "core"), in_pairs)
    qg = exchange(qg_packed)
    kv_other = lax.ppermute(kv, "core", swap)
    kv_first, kv_second, qg, kv_other = lax.optimization_barrier(
        (kv_first, kv_second, qg, kv_other)
    )
    sides_own = join(kv_first, kv_second)
    sides_other = lax.ppermute(sides_own, "core", swap)
    oq, own, other = attend(plan, qg, (kv, sides_own, kv_other, sides_other))
    mine = lax.ppermute(other, "core", swap)
    to_first, to_second, here = sides(own, mine)
    from_first = lax.ppermute(to_first, ("z", "core"), in_pairs)
    from_second = lax.ppermute(to_second, ("z", "core"), out_pairs)
    back_oq = exchange(oq)
    total = finish(here, from_first, from_second)
    dquery, out = unpack(back_oq)
    dkey, dvalue = unpack(exchange(total))
    return out, dquery, dkey, dvalue


def solution(mesh):
    inner = Mesh(mesh.devices.reshape(16, 2, 2, 4, 2), AXES)
    return jax.shard_map(
        on_device,
        mesh=inner,
        in_specs=(P(AXES, None),) * 4 + (P(), P()),
        out_specs=(P(AXES, None),) * 4,
        check_vma=False,
    )
```

```python
import functools

import jax
import jax.numpy as jnp
from jax import lax
from jax.experimental import pallas as pl
from jax.experimental.pallas import tpu as pltpu
from jax.sharding import Mesh, PartitionSpec as P

H = 16
E = 64
BLK = 128
NNB = 8
PLANES = 3
PACK_STEPS = 4
LOG2E = 1.4426950408889634

AXES = ("z", "yl", "yh", "x", "core")
HEADS = ("yl", "yh", "x")
VMEM = pltpu.VMEM


def pack_kernel(a_hbm, b_hbm, o_hbm, a_buf, b_buf, o_buf, in_sems, out_sems):
    wide = 2 * E * H // 2 // PACK_STEPS
    tall = H // PACK_STEPS

    def fetch(src, dst, which, i):
        cols = pl.ds(i * wide, wide)
        return pltpu.make_async_copy(src.at[:, cols], dst.at[:, cols], in_sems.at[which, i])

    def put(i):
        rows = pl.ds(i * tall, tall)
        return pltpu.make_async_copy(o_buf.at[rows], o_hbm.at[rows], out_sems.at[i])

    for i in range(PACK_STEPS):
        fetch(a_hbm, a_buf, 0, i).start()
        fetch(b_hbm, b_buf, 1, i).start()
    for i in range(PACK_STEPS):
        fetch(a_hbm, a_buf, 0, i).wait()
        fetch(b_hbm, b_buf, 1, i).wait()
        for pair in range(i * tall // 2, (i + 1) * tall // 2):
            cols = slice(pair * 2 * E, (pair + 1) * 2 * E)
            a = a_buf[:, cols]
            b = b_buf[:, cols]
            o_buf[2 * pair] = jnp.concatenate([a[:, :E], b[:, :E]], axis=1)
            o_buf[2 * pair + 1] = jnp.concatenate([a[:, E:], b[:, E:]], axis=1)
        put(i).start()
    for i in range(PACK_STEPS):
        put(i).wait()


def pack(a, b):
    rows, width = a.shape
    joined = (H, rows, 2 * E)
    return pl.pallas_call(
        pack_kernel,
        out_shape=jax.ShapeDtypeStruct(joined, a.dtype),
        in_specs=[pl.BlockSpec(memory_space=pl.ANY)] * 2,
        out_specs=pl.BlockSpec(memory_space=pl.ANY),
        scratch_shapes=[
            pltpu.VMEM((rows, width), a.dtype),
            pltpu.VMEM((rows, width), a.dtype),
            pltpu.VMEM(joined, a.dtype),
            pltpu.SemaphoreType.DMA((2, PACK_STEPS)),
            pltpu.SemaphoreType.DMA((PACK_STEPS,)),
        ],
        cost_estimate=pl.CostEstimate(flops=0, bytes_accessed=1 << 20, transcendentals=0),
        name="pack",
    )(a, b)


def unpack_kernel(i_ref, a_ref, b_ref):
    for pair in range(H // 2):
        cols = slice(pair * 2 * E, (pair + 1) * 2 * E)
        even = i_ref[2 * pair]
        odd = i_ref[2 * pair + 1]
        a_ref[:, cols] = jnp.concatenate([even[:, :E], odd[:, :E]], axis=1)
        b_ref[:, cols] = jnp.concatenate([even[:, E:], odd[:, E:]], axis=1)


def unpack(joined):
    rows = joined.shape[1]
    shape = jax.ShapeDtypeStruct((rows, H * E), joined.dtype)
    return pl.pallas_call(
        unpack_kernel,
        out_shape=(shape, shape),
        in_specs=[pl.BlockSpec(memory_space=VMEM)],
        out_specs=[pl.BlockSpec(memory_space=VMEM)] * 2,
        compiler_params=pltpu.CompilerParams(vmem_limit_bytes=4 << 20),
        cost_estimate=pl.CostEstimate(flops=0, bytes_accessed=1 << 20, transcendentals=0),
        name="unpack",
    )(joined)


def sides_kernel(own_ref, mine_ref, before_ref, after_ref, here_ref):
    blocks = before_ref.shape[0]

    @pl.loop(0, blocks)
    def _(i):
        before = own_ref[i] + mine_ref[i].astype(jnp.float32)
        after = own_ref[2 * blocks + i] + mine_ref[2 * blocks + i].astype(jnp.float32)
        before_ref[i] = before.astype(before_ref.dtype)
        after_ref[i] = after.astype(after_ref.dtype)
        here_ref[i] = own_ref[blocks + i] + mine_ref[blocks + i].astype(jnp.float32)


def sides(own, mine):
    shape = jax.ShapeDtypeStruct((own.shape[0] // PLANES,) + own.shape[1:], mine.dtype)
    return pl.pallas_call(
        sides_kernel,
        out_shape=(shape, shape, jax.ShapeDtypeStruct(shape.shape, jnp.float32)),
        in_specs=[pl.BlockSpec(memory_space=VMEM)] * 2,
        out_specs=[pl.BlockSpec(memory_space=VMEM)] * 3,
        compiler_params=pltpu.CompilerParams(vmem_limit_bytes=8 << 20),
        cost_estimate=pl.CostEstimate(flops=0, bytes_accessed=4 << 20, transcendentals=0),
        name="sides",
    )(own, mine)


def finish_kernel(here_ref, first_ref, second_ref, o_hbm, o_buf, sems):
    blocks = here_ref.shape[0]
    tall = blocks // PACK_STEPS

    def put(i):
        rows = pl.ds(i * tall, tall)
        return pltpu.make_async_copy(o_buf.at[rows], o_hbm.at[rows], sems.at[i])

    for i in range(PACK_STEPS):
        for j in range(i * tall, (i + 1) * tall):
            total = first_ref[j].astype(jnp.float32) + second_ref[j].astype(jnp.float32)
            total = here_ref[j] + total
            o_buf[j] = total.astype(o_buf.dtype)
        put(i).start()
    for i in range(PACK_STEPS):
        put(i).wait()


def finish(here, first, second):
    return pl.pallas_call(
        finish_kernel,
        out_shape=jax.ShapeDtypeStruct(first.shape, first.dtype),
        in_specs=[pl.BlockSpec(memory_space=VMEM)] * 3,
        out_specs=pl.BlockSpec(memory_space=pl.ANY),
        scratch_shapes=[pltpu.VMEM(first.shape, first.dtype), pltpu.SemaphoreType.DMA((PACK_STEPS,))],
        compiler_params=pltpu.CompilerParams(vmem_limit_bytes=8 << 20),
        cost_estimate=pl.CostEstimate(flops=0, bytes_accessed=3 << 20, transcendentals=0),
        name="finish",
    )(here, first, second)


def plan_kernel(place, nbr, cnt, plan, fill):
    z, core = place()
    blocks = plan.shape[0]
    plane_blocks = 2 * blocks
    all_blocks = cnt.shape[0]
    first = (z - 1) * plane_blocks
    shift = plane_blocks.bit_length() - 1
    assert plane_blocks == 1 << shift and all_blocks & (all_blocks - 1) == 0

    def block_of(s):
        return z * plane_blocks + 2 * s + core

    for c in range(NNB + 2):
        fill[c] = 0

    @pl.loop(0, blocks)
    def _(s):
        c = cnt[block_of(s)]
        fill[c + 1] += 1

    for c in range(2, NNB + 1):
        fill[c] += fill[c - 1]

    @pl.loop(0, blocks)
    def _(s):
        b = block_of(s)
        c = cnt[b]
        at = fill[c]
        fill[c] += 1
        plan[at, NNB] = s
        plan[at, NNB + 1] = c
        for j in range(NNB):
            rel = (nbr[j, b] - first) & (all_blocks - 1)
            plane = rel >> shift
            slot = plane + (rel & 1) * (PLANES - 1 - 2 * plane)
            side = (rel + core) & 1
            within = (rel & (plane_blocks - 1)) >> 1
            plan[at, j] = (side * PLANES + slot) * blocks + within


def plan_blocks(place, nbr_t, counts, blocks):
    return pl.pallas_call(
        functools.partial(plan_kernel, place),
        out_shape=jax.ShapeDtypeStruct((blocks, 2 * NNB), jnp.int32),
        in_specs=[pl.BlockSpec(memory_space=pltpu.SMEM)] * 2,
        out_specs=pl.BlockSpec(memory_space=pltpu.SMEM),
        scratch_shapes=[pltpu.SMEM((NNB + 2,), jnp.int32)],
        compiler_params=pltpu.CompilerParams(vmem_limit_bytes=1 << 20),
        cost_estimate=pl.CostEstimate(flops=0, bytes_accessed=1 << 20, transcendentals=0),
        name="plan",
    )(nbr_t, counts)


def join_kernel(a_ref, b_ref, o_ref):
    blocks = a_ref.shape[0]
    o_ref[:blocks] = a_ref[...]
    o_ref[blocks:] = b_ref[...]


def join(a, b):
    return pl.pallas_call(
        join_kernel,
        out_shape=jax.ShapeDtypeStruct((2 * a.shape[0],) + a.shape[1:], a.dtype),
        in_specs=[pl.BlockSpec(memory_space=VMEM)] * 2,
        out_specs=pl.BlockSpec(memory_space=VMEM),
        compiler_params=pltpu.CompilerParams(vmem_limit_bytes=4 << 20),
        cost_estimate=pl.CostEstimate(flops=0, bytes_accessed=2 << 20, transcendentals=0),
        name="join",
    )(a, b)


def attend_group(group, slots, qg_ref, win, acc, st, jn, oq_ref):
    low = lax.broadcasted_iota(jnp.int32, (BLK, 2 * E), 1) < E
    members = range(len(group))
    both = []
    where = []
    for s, used, found in group:
        qg = qg_ref[s]
        zero = jnp.zeros_like(qg)
        both.append(
            jnp.concatenate(
                [jnp.where(low, qg * jnp.bfloat16(0.125), zero), jnp.where(low, zero, qg)], axis=0
            )
        )
        where.append([found(j) for j in range(slots)])
    rows = [slice(j * BLK, (j + 1) * BLK) for j in range(slots)]
    everything = slice(0, slots * BLK)
    live = [[j == 0 or j < used for j in range(slots)] for _, used, _ in group]
    tops = []
    for m in members:
        keys = jnp.concatenate([win[where[m][j]] for j in range(slots)], axis=0)
        st[m, everything] = lax.dot_general(
            keys, both[m], (((1,), (1,)), ((), ())), preferred_element_type=jnp.float32
        )
        top = [jnp.max(st[m, rows[j], :BLK], axis=0, keepdims=True) for j in range(slots)]
        highest = top[0]
        for j in range(1, slots):
            highest = jnp.maximum(highest, jnp.where(live[m][j], top[j], -1e30))
        tops.append(
            [highest if j == 0 else jnp.where(live[m][j], highest, 1e30) for j in range(slots)]
        )
    inverse = []
    delta = []
    for m in members:
        total = jnp.zeros((1, BLK), jnp.float32)
        mixed = jnp.zeros((1, BLK), jnp.float32)
        for j in range(slots):
            raised = jnp.exp2((st[m, rows[j], :BLK] - tops[m][j]) * LOG2E)
            st[m, rows[j], :BLK] = raised
            total = total + jnp.sum(raised, axis=0, keepdims=True)
            mixed = mixed + jnp.sum(raised * st[m, rows[j], BLK:], axis=0, keepdims=True)
        inverse.append(1.0 / total)
        delta.append(mixed * inverse[m])
    for m in members:
        for j in range(slots):
            probability = st[m, rows[j], :BLK] * inverse[m]
            dscore = probability * (st[m, rows[j], BLK:] - delta[m])
            jn[m, rows[j], :BLK] = dscore.astype(jnp.bfloat16)
            jn[m, rows[j], BLK:] = probability.astype(jnp.bfloat16)
        joined = jn[m, everything]
        parts = jnp.dot(joined, both[m], preferred_element_type=jnp.float32)
        for j in range(slots):
            acc[where[m][j]] += parts[rows[j]]
        turned = jnp.concatenate([win[where[m][j]].T for j in range(slots)], axis=1)
        sums = jnp.dot(turned, joined, preferred_element_type=jnp.float32)
        result = jnp.concatenate([sums[:E, :BLK] * 0.125, sums[E:, BLK:]], axis=0)
        oq_ref[group[m][0]] = result.T.astype(oq_ref.dtype)


def entry(plan, at, j):
    return plan[at, j]


def attend_kernel(variants, size, plan, qg_ref, *rest):
    kv_refs = rest[:4]
    oq_ref, own_ref, other_ref = rest[4:7]
    win, acc, st, jn, sems = rest[7:]
    blocks = qg_ref.shape[0]
    pieces = (
        (1, 0, 0), (0, 0, 1), (2, 1, 1), (4, 0, 2), (3, 0, 3), (5, 1, 3)
    )
    copies = [
        pltpu.make_async_copy(
            kv_refs[which].at[pl.ds(part * blocks, blocks)],
            win.at[pl.ds(slot * blocks, blocks)],
            sems.at[slot],
        )
        for slot, part, which in pieces
    ]
    for copy in copies:
        copy.start()

    @pl.loop(0, 2 * PLANES * blocks)
    def _(i):
        acc[i] = jnp.zeros_like(acc[i])

    for copy in copies:
        copy.wait()

    @pl.loop(0, blocks // size)
    def _(i):
        group = []
        for m in range(size):
            at = i * size + m
            group.append((plan[at, NNB], plan[at, NNB + 1], functools.partial(entry, plan, at)))
        most = group[-1][1]
        before = 0
        for slots in variants:

            @pl.when((most > before) & (most <= slots))
            def _(slots=slots):
                attend_group(group, slots, qg_ref, win, acc, st, jn, oq_ref)

            before = slots

    @pl.loop(0, PLANES * blocks)
    def _(i):
        own_ref[i] = acc[i]
        other_ref[i] = acc[PLANES * blocks + i].astype(other_ref.dtype)


def attend(plan, qg, kvs, variants=(1, 2, 3, 4, 5, 6, 7, 8), size=4):
    blocks = qg.shape[0]
    tile = (BLK, 2 * E)
    return pl.pallas_call(
        functools.partial(attend_kernel, variants, size),
        out_shape=(
            jax.ShapeDtypeStruct((blocks,) + tile, jnp.bfloat16),
            jax.ShapeDtypeStruct((PLANES * blocks,) + tile, jnp.float32),
            jax.ShapeDtypeStruct((PLANES * blocks,) + tile, jnp.bfloat16),
        ),
        in_specs=[pl.BlockSpec(memory_space=pltpu.SMEM), pl.BlockSpec(memory_space=VMEM)]
        + [pl.BlockSpec(memory_space=pltpu.HBM)] * 4,
        out_specs=[pl.BlockSpec(memory_space=VMEM)] * 3,
        scratch_shapes=[
            pltpu.VMEM((6 * blocks,) + tile, jnp.bfloat16),
            pltpu.VMEM((6 * blocks,) + tile, jnp.float32),
            pltpu.VMEM((size, NNB * BLK, 2 * BLK), jnp.float32),
            pltpu.VMEM((size, NNB * BLK, 2 * BLK), jnp.bfloat16),
            pltpu.SemaphoreType.DMA((6,)),
        ],
        compiler_params=pltpu.CompilerParams(vmem_limit_bytes=32 << 20),
        cost_estimate=pl.CostEstimate(
            flops=2 * 5 * blocks * 5 * BLK * BLK * E,
            bytes_accessed=8 << 20,
            transcendentals=blocks * 5 * BLK * BLK,
        ),
        name="attend",
    )(plan, qg, *kvs)


def on_device(query, key, value, grad_out, neighbour, counts):
    planes = lax.axis_size("z")
    out_pairs = []
    in_pairs = []
    for i in range(planes):
        for core in range(2):
            ahead = (i + 1 - 2 * core) % planes
            out_pairs.append((2 * i + core, 2 * ahead + core))
            in_pairs.append((2 * ahead + core, 2 * i + core))
    swap = [(0, 1), (1, 0)]

    def place():
        return lax.axis_index("z"), lax.axis_index("core")

    def exchange(packed):
        return lax.all_to_all(packed, HEADS, split_axis=0, concat_axis=0, tiled=True)

    kv = exchange(pack(key, value))
    blocks = kv.shape[0]
    plan = plan_blocks(place, neighbour.T, counts, blocks)
    kv, qg_packed, plan = lax.optimization_barrier((kv, pack(query, grad_out), plan))
    kv_first = lax.ppermute(kv, ("z", "core"), out_pairs)
    kv_second = lax.ppermute(kv, ("z", "core"), in_pairs)
    qg = exchange(qg_packed)
    kv_other = lax.ppermute(kv, "core", swap)
    kv_first, kv_second, qg, kv_other = lax.optimization_barrier(
        (kv_first, kv_second, qg, kv_other)
    )
    sides_own = join(kv_first, kv_second)
    sides_other = lax.ppermute(sides_own, "core", swap)
    oq, own, other = attend(plan, qg, (kv, sides_own, kv_other, sides_other))
    mine = lax.ppermute(other, "core", swap)
    to_first, to_second, here = sides(own, mine)
    from_first = lax.ppermute(to_first, ("z", "core"), in_pairs)
    from_second = lax.ppermute(to_second, ("z", "core"), out_pairs)
    back_oq = exchange(oq)
    total = finish(here, from_first, from_second)
    dquery, out = unpack(back_oq)
    dkey, dvalue = unpack(exchange(total))
    return out, dquery, dkey, dvalue


def solution(mesh):
    inner = Mesh(mesh.devices.reshape(16, 2, 2, 4, 2), AXES)
    return jax.shard_map(
        on_device,
        mesh=inner,
        in_specs=(P(AXES, None),) * 4 + (P(), P()),
        out_specs=(P(AXES, None),) * 4,
        check_vma=False,
    )
```
